128 devices in a mesh: dp: 8 (over z, core), shard: 16 (over x, y).
Axes of the slice: x: 4, y: 4, z: 4, core: 2. Of those that a mesh axis runs over, the one named last changes fastest.
Arguments:
- tokens: bfloat16 [4096, 4096], P(('dp', 'shard')), may hold values from -6 to 6
- cotangent: bfloat16 [4096, 4096], P(('dp', 'shard')), may hold values from -6 to 6
- w_up: bfloat16 [4096, 14336], P('shard', 'dp'), may hold values from -0.09375 to 0.09375
- w_down: bfloat16 [14336, 4096], P('dp', 'shard'), may hold values from -0.046875 to 0.046875
- delta: float32 [512, 128, 128], P(('dp', 'shard')), may hold values from -0.5 to 0.5
- first_moment: float32 [512, 128, 128], P(('dp', 'shard')), may hold values from -1.8 to 1.8
- second_moment: float32 [512, 128, 128], P(('dp', 'shard')), may hold values from 0.02 to 0.3
- blk_row: int32 [512], replicated, may hold values from 0 to 31
- blk_col: int32 [512], replicated, may hold values from 0 to 111, as said below
- live: int32 [512], replicated, may hold values from 0 to 1, as said below
Outputs:
- layer_out: bfloat16 [4096, 4096], P(('dp', 'shard'))
- new_delta: float32 [512, 128, 128], P(('dp', 'shard'))
- new_first: float32 [512, 128, 128], P(('dp', 'shard'))
- new_second: float32 [512, 128, 128], P(('dp', 'shard'))
The draws below stay inside these ranges and needn't reach their ends.
Inputs may be any that keep to these rules, and one draw needn't show every extreme that they name: `blk_col`: slots j to j + 16 * 4 - 1 with j a multiple of 64 name distinct blocks, all with block columns from (j // 64) * 14 to that plus 14 - 1. The live slots of each device come first among its 4 slots; some device has all 4 live.
All inputs are finite; a program needn't handle non-finite values.
Results may differ from the reference program's by a relative error of at most 0.014.
Values may be sent and summed in bfloat16 or wider, within the bound.
No kernel may reach another device: no remote copies, remote signals or barrier semaphores. Data moves between devices by JAX's collectives and lax.ppermute only.
A program may use at most 192 MiB of HBM per device.

```python
import math
import jax
import jax.numpy as jnp
from jax import lax

D = 4096
FF = 14336
BLK = 128
OWN = 4
BLOCK_ROWS = 32
BLOCK_COLS = 14
SLOTS = 512
TOKENS = 4096
N_DP = 8
N_SHARD = 16
DEVICES = 128


def pick_cells(key):
    base = jax.random.fold_in(key, 7)
    keys = jax.random.split(base, N_DP)
    return jax.vmap(lambda k: jax.random.permutation(k, BLOCK_ROWS * BLOCK_COLS)[:N_SHARD * OWN])(keys)


def draw_blk_row(key, part):
    cells = pick_cells(key)
    return (cells // BLOCK_COLS).reshape(-1).astype(jnp.int32)


def draw_blk_col(key, part):
    cells = pick_cells(key)
    offsets = jnp.arange(N_DP, dtype=jnp.int32)[:, None] * BLOCK_COLS
    return (cells % BLOCK_COLS + offsets).reshape(-1).astype(jnp.int32)


def draw_live(key, part):
    counts = jax.random.randint(jax.random.fold_in(key, 3), (DEVICES,), 0, OWN + 1)
    chosen = jax.random.randint(jax.random.fold_in(key, 5), (), 0, DEVICES)
    counts = jnp.where(jnp.arange(DEVICES) == chosen, OWN, counts)
    flags = jnp.arange(OWN, dtype=jnp.int32)[None, :] < counts[:, None]
    return flags.reshape(-1).astype(jnp.int32)


def shard_levels(key, shape, shards, low, largest):
    def one(position, parts):
        draws = jax.random.uniform(jax.random.fold_in(jax.random.fold_in(key, 6), position), (parts,), jnp.float32, low / len(shards), largest / len(shards))
        return jnp.repeat(jnp.exp(draws), shape[position] // parts).reshape((-1,) + (1,) * (len(shape) - position - 1))

    loudness = one(*shards[0])
    for cut in shards[1:]:
        loudness = loudness * one(*cut)
    return loudness


def centred(rng, dims, scale, reach, pieces=(), held_as=jnp.bfloat16):
    entries = jax.random.normal(rng, dims, jnp.float32) * scale
    if len(pieces) > 0:
        entries = shard_levels(rng, dims, pieces, -0.22, 0.18) * entries
    return jnp.clip(entries, min=-reach, max=reach).astype(held_as)


def setup_inputs(seed: int = 0) -> dict:
    seeds = jax.random.split(jax.random.key(seed), 11)
    tokens = centred(seeds[0], (TOKENS, D), 1.0, 6.0, ((0, 128),))
    cotangent = centred(seeds[1], (TOKENS, D), 1.0, 6.0, ((0, 128),))
    w_up = centred(seeds[2], (D, FF), D ** -0.5, 0.09375, ((0, 16), (1, 8)))
    w_down = centred(seeds[3], (FF, D), FF ** -0.5, 0.046875, ((0, 8), (1, 16)))
    delta = centred(seeds[4], (SLOTS, BLK, BLK), BLK ** -0.5, 0.5, ((0, 128),), jnp.float32)
    first_moment = centred(seeds[5], (SLOTS, BLK, BLK), 0.3, 1.8, ((0, 128),), jnp.float32)
    second_moment = jnp.clip(jnp.exp(math.log(0.3) - 2.7080503 * jax.random.uniform(seeds[6], (SLOTS, BLK, BLK), jnp.float32) ** shard_levels(seeds[6], (SLOTS, BLK, BLK), ((0, 128),), -0.2, 0.2)), 0.02, 0.3)
    blk_row = draw_blk_row(jax.random.fold_in(seeds[10], 71), 0)
    blk_col = draw_blk_col(jax.random.fold_in(seeds[10], 71), 0)
    live = draw_live(jax.random.fold_in(seeds[10], 71), 0)
    return dict(tokens=tokens, cotangent=cotangent, w_up=w_up, w_down=w_down, delta=delta, first_moment=first_moment, second_moment=second_moment, blk_row=blk_row, blk_col=blk_col, live=live)


def reference(tokens, cotangent, w_up, w_down, delta, first_moment, second_moment, blk_row, blk_col, live):
    blocks = delta.astype(jnp.bfloat16)
    alive = live.astype(jnp.float32)
    pre = jnp.dot(tokens, w_up, preferred_element_type=jnp.float32)

    def add_block(total, item):
        block, row_idx, col_idx, flag = item
        inputs = lax.dynamic_slice_in_dim(tokens, (row_idx * BLK).astype(jnp.int32), BLK, 1)
        term = jnp.dot(inputs, block, preferred_element_type=jnp.float32) * flag
        start = (col_idx * BLK).astype(jnp.int32)
        current = lax.dynamic_slice_in_dim(total, start, BLK, 1)
        return (lax.dynamic_update_slice_in_dim(total, current + term, start, 1), None)
    pre, _ = lax.scan(add_block, pre, (blocks, blk_row, blk_col, alive))
    hidden = jax.nn.silu(pre).astype(jnp.bfloat16)
    layer_out = jnp.dot(hidden, w_down, preferred_element_type=jnp.float32).astype(jnp.bfloat16)
    back = lax.dot_general(cotangent, w_down, (((1,), (1,)), ((), ())), preferred_element_type=jnp.float32)
    sigma = jax.nn.sigmoid(pre)
    dpre = (back * sigma * (1.0 + pre * (1.0 - sigma))).astype(jnp.bfloat16)
    factor = 1.0 / jnp.sqrt(jnp.float32(TOKENS))

    def block_grad(item):
        row_idx, col_idx, flag = item
        inputs = lax.dynamic_slice_in_dim(tokens, (row_idx * BLK).astype(jnp.int32), BLK, 1)
        slope = lax.dynamic_slice_in_dim(dpre, (col_idx * BLK).astype(jnp.int32), BLK, 1)
        prod = lax.dot_general(inputs, slope, (((0,), (0,)), ((), ())), preferred_element_type=jnp.float32)
        return prod * flag * factor
    grads = lax.map(block_grad, (blk_row, blk_col, alive))
    new_first = 0.9 * first_moment + 0.1 * grads
    new_second = 0.95 * second_moment + 0.05 * grads * grads
    corrected_first = new_first / (1.0 - 0.9 ** 10)
    corrected_second = new_second / (1.0 - 0.95 ** 10)
    new_delta = delta - 0.01 * corrected_first / (jnp.sqrt(corrected_second) + 1e-08)
    return (layer_out, new_delta, new_first, new_second)
```

```python
import math

import jax
import jax.numpy as jnp
from jax import lax
from jax.experimental import pallas as pl
from jax.experimental.pallas import tpu as pltpu
from jax.sharding import Mesh
from jax.sharding import PartitionSpec as P


DEVICE = ("z", "c", "x", "y")
SHARD = ("x", "y")
DP = ("z", "c")
SIDE = 128
F32 = jnp.float32
BF16 = jnp.bfloat16


def shift(value, axis, by):
    return lax.ppermute(value, axis, [(k, (k + by) % 4) for k in range(4)])


def swap_cores(value):
    return lax.ppermute(value, "c", [(0, 1), (1, 0)])


def struct(shape, dtype):
    return jax.ShapeDtypeStruct(shape, dtype)


def cost(flops, nbytes):
    return pl.CostEstimate(flops=flops, bytes_accessed=nbytes, transcendentals=0)


def ring(piece, axis):
    half = piece.shape[0] // 2
    before = shift(piece, axis, 1)
    after = shift(piece, axis, -1)
    top = shift(before[:half], axis, 1)
    bottom = shift(after[half:], axis, -1)
    return piece, before, top, bottom, after


def over_dp(unit):
    mine = jnp.concatenate([unit] + [shift(unit, "z", k) for k in range(1, 4)], axis=0)
    return mine, swap_cores(mine)


def wrap(index):
    return lax.rem(index + 8, 4)


def prepare_kernel(tokens, cotangent, t0, t1, t2, t3, c0, c1, c2, c3):
    x, y = lax.axis_index("x"), lax.axis_index("y")
    for k, out in enumerate((t0, t1, t2, t3)):
        out[...] = tokens[:, pl.ds(pl.multiple_of(wrap(x + k) * 1024, 1024), 1024)]
    for k, out in enumerate((c0, c1, c2, c3)):
        for i in range(4):
            begin = pl.multiple_of(i * 1024 + wrap(y + k) * 256, 256)
            out[:, i * 256 : (i + 1) * 256] = cotangent[:, pl.ds(begin, 256)]


def prepare(tokens, cotangent):
    rows = tokens.shape[0]
    outs = pl.pallas_call(
        prepare_kernel,
        out_shape=[struct((rows, 1024), BF16)] * 8,
        cost_estimate=cost(0, 4 * tokens.size * 2),
    )(tokens, cotangent)
    return outs[:4], outs[4:]


def gather_rows(mine, other, lhs, position):
    for group in range(4):
        for core, ref in enumerate((mine, other)):
            for zr in range(4):
                to = group * 256 + core * 128 + zr * 32
                at = zr * 128 + group * 32
                for k in range(4):
                    begin = pl.multiple_of(wrap(position - k) * 256, 256)
                    lhs[to : to + 32, k * 256 : (k + 1) * 256] = ref[
                        at : at + 32, pl.ds(begin, 256)
                    ]


def up_kernel(mine, other, w0, w1, w2a, w2b, w3, o0, o1, o2, o3, lhs):
    @pl.when(pl.program_id(0) == 0)
    def _():
        gather_rows(mine, other, lhs, lax.axis_index("y"))

    total = jnp.dot(lhs[:, :256], w0[...], preferred_element_type=F32)
    total += jnp.dot(lhs[:, 256:512], w1[...], preferred_element_type=F32)
    total += jnp.dot(lhs[:, 512:640], w2a[...], preferred_element_type=F32)
    total += jnp.dot(lhs[:, 640:768], w2b[...], preferred_element_type=F32)
    total += jnp.dot(lhs[:, 768:], w3[...], preferred_element_type=F32)
    for group, out in enumerate((o0, o1, o2, o3)):
        out[...] = total[group * 256 : (group + 1) * 256].astype(BF16)


def up_partial(mine, other, pieces):
    width = pieces[0].shape[1]
    whole = pl.BlockSpec((512, 1024), lambda n: (0, 0))
    return pl.pallas_call(
        up_kernel,
        grid=(width // 256,),
        in_specs=[whole, whole]
        + [pl.BlockSpec((p.shape[0], 256), lambda n: (0, n)) for p in pieces],
        out_specs=[pl.BlockSpec((256, 256), lambda n: (0, n))] * 4,
        out_shape=[struct((256, width), BF16)] * 4,
        scratch_shapes=[pltpu.VMEM((1024, 1024), BF16)],
        cost_estimate=cost(2 * 1024 * 1024 * width, 4 * 1024 * width),
    )(mine, other, *pieces)


def back_kernel(mine, other, w0, w1, w2, w3, o0, o1, o2, o3, lhs):
    @pl.when(pl.program_id(0) == 0)
    def _():
        gather_rows(mine, other, lhs, lax.axis_index("x"))

    total = None
    for k, w in enumerate((w0, w1, w2, w3)):
        term = lax.dot_general(
            lhs[:, k * 256 : (k + 1) * 256],
            w[...],
            (((1,), (1,)), ((), ())),
            preferred_element_type=F32,
        )
        total = term if total is None else total + term
    for group, out in enumerate((o0, o1, o2, o3)):
        out[...] = total[group * 256 : (group + 1) * 256].astype(BF16)


def back_partial(mine, other, pieces):
    width = pieces[0].shape[0]
    whole = pl.BlockSpec((512, 1024), lambda n: (0, 0))
    return pl.pallas_call(
        back_kernel,
        grid=(width // 256,),
        in_specs=[whole, whole] + [pl.BlockSpec((256, 256), lambda n: (n, 0))] * 4,
        out_specs=[pl.BlockSpec((256, 256), lambda n: (0, n))] * 4,
        out_shape=[struct((256, width), BF16)] * 4,
        scratch_shapes=[pltpu.VMEM((1024, 1024), BF16)],
        cost_estimate=cost(2 * 1024 * 1024 * width, 4 * 1024 * width),
    )(mine, other, *pieces)


def out_kernel(h0, h1, h2a, h2b, h3, w0, w1, w2, w3, p0, p1, lhs):
    n = pl.program_id(0)

    @pl.when(n == 0)
    def _():
        lhs[:256] = h0[...]
        lhs[256:512] = h1[...]
        lhs[512:640] = h2a[...]
        lhs[640:768] = h2b[...]
        lhs[768:] = h3[...]

    for pair, (a, b) in enumerate(((w0, w1), (w2, w3))):
        both = jnp.concatenate([a[...], b[...]], axis=1)
        total = jnp.dot(lhs[...], both, preferred_element_type=F32).astype(BF16)
        for half in range(2):
            at = pl.multiple_of((2 * pair + half) * 256 + n * 128, 128)
            for core, out in enumerate((p0, p1)):
                for zr in range(4):
                    for group in range(4):
                        row = group * 256 + core * 128 + zr * 32
                        out[zr, group, :, pl.ds(at, 128)] = total[
                            row : row + 32, half * 128 : (half + 1) * 128
                        ]


def out_partial(hidden, pieces):
    width = pieces[0].shape[0]
    held = pl.BlockSpec((4, 4, 32, 1024), lambda n: (0, 0, 0, 0))
    return pl.pallas_call(
        out_kernel,
        grid=(2,),
        in_specs=[pl.BlockSpec(h.shape, lambda n: (0, 0)) for h in hidden]
        + [pl.BlockSpec((width, 128), lambda n: (0, n))] * 4,
        out_specs=[held, held],
        out_shape=[struct((4, 4, 32, 1024), BF16)] * 2,
        scratch_shapes=[pltpu.VMEM((1024, width), BF16)],
        cost_estimate=cost(2 * 1024 * 1024 * width, 4 * 1024 * width),
    )(*hidden, *pieces)


def slot_of(i, j, k, sign):
    x, y = lax.axis_index("x"), lax.axis_index("y")
    group = lax.axis_index("z") * 2 + lax.axis_index("c")
    return group * 64 + wrap(x + sign * i) * 16 + wrap(y + sign * j) * 4 + k


def place_of(slot, row, col, live):
    group = lax.axis_index("z") * 2 + lax.axis_index("c")
    at_row = pl.multiple_of(row[slot] * SIDE, SIDE)
    at_col = pl.multiple_of((col[slot] - group * 14) * SIDE, SIDE)
    return at_row, at_col, live[slot].astype(F32)


def terms_kernel(row, col, live, mine, other, b0, b1, b2, b3, terms, flipped):
    terms[...] = jnp.zeros_like(terms)
    for i, ref in enumerate((b0, b1, b2, b3)):
        for j in range(4):
            for k in range(4):
                at_row, at_col, flag = place_of(slot_of(i, j, k, -1), row, col, live)
                block = ref[j * 4 + k]
                for core, x_ref in enumerate((mine, other)):
                    term = jnp.dot(
                        x_ref[:, pl.ds(at_row, SIDE)], block, preferred_element_type=F32
                    )
                    here = (pl.ds(core * 128, 128), pl.ds(at_col, SIDE))
                    terms[here] = terms[here] + term * flag
    for r in range(32):
        for core, x_ref in enumerate((mine, other)):
            flipped[r * 128 : (r + 1) * 128, core * 128 : (core + 1) * 128] = x_ref[
                :, r * 128 : (r + 1) * 128
            ].T


def slot_terms(row, col, live, mine, other, blocks, width):
    smem = pl.BlockSpec(memory_space=pltpu.SMEM)
    vmem = pl.BlockSpec(memory_space=pltpu.VMEM)
    return pl.pallas_call(
        terms_kernel,
        in_specs=[smem] * 3 + [vmem] * 6,
        out_specs=[vmem, vmem],
        out_shape=[struct((256, width), F32), struct((4096, 256), BF16)],
        cost_estimate=cost(64 * 2 * 256 * 128 * 128, 8 << 20),
    )(row, col, live, mine, other, *blocks)


def grads_kernel(factor, row, col, live, pre, r0, r1, r2, r3, flipped, g0, g1, g2, g3, dpre):
    for n in range(pre.shape[1] // 256):
        at = slice(n * 256, (n + 1) * 256)
        back = r0[:, at].astype(F32) + r1[:, at].astype(F32)
        back = back + (r2[:, at].astype(F32) + r3[:, at].astype(F32))
        value = pre[:, at]
        sigma = jax.nn.sigmoid(value)
        dpre[:, at] = (back * sigma * (1.0 + value * (1.0 - sigma))).astype(BF16)
    for i, out in enumerate((g0, g1, g2, g3)):
        for j in range(4):
            for k in range(4):
                at_row, at_col, flag = place_of(slot_of(i, j, k, 1), row, col, live)
                grad = jnp.dot(
                    flipped[pl.ds(at_row, SIDE), :],
                    dpre[:, pl.ds(at_col, SIDE)],
                    preferred_element_type=F32,
                )
                out[j * 4 + k] = (grad * (flag * factor)).astype(BF16)


def slot_grads(row, col, live, pre, back, flipped, factor):
    smem = pl.BlockSpec(memory_space=pltpu.SMEM)
    vmem = pl.BlockSpec(memory_space=pltpu.VMEM)

    def kernel(*refs):
        grads_kernel(factor, *refs)

    return pl.pallas_call(
        kernel,
        in_specs=[smem] * 3 + [vmem] * 6,
        out_specs=[vmem] * 4,
        out_shape=[struct((16, SIDE, SIDE), BF16)] * 4,
        scratch_shapes=[pltpu.VMEM(pre.shape, BF16)],
        cost_estimate=cost(64 * 2 * 256 * 128 * 128, 8 << 20),
    )(row, col, live, pre, *back, flipped)


def finish_kernel(r0, r1, r2, r3, out):
    x, y = lax.axis_index("x"), lax.axis_index("y")
    for j, ref in enumerate((r0, r1, r2, r3)):
        for i in range(4):
            begin = pl.multiple_of(wrap(x - i) * 1024 + wrap(y + j) * 256, 256)
            out[:, pl.ds(begin, 256)] = ref[:, i * 256 : (i + 1) * 256]


def finish(pieces):
    return pl.pallas_call(
        finish_kernel,
        out_shape=struct((32, 4096), BF16),
        cost_estimate=cost(0, 1 << 19),
    )(*pieces)


def total_of(pieces):
    total = pieces[0].astype(F32)
    for piece in pieces[1:]:
        total = total + piece.astype(F32)
    return total


def on_device(
    tokens, cotangent, w_up, w_down, delta, first_moment, second_moment, blk_row, blk_col, live
):
    width = w_up.shape[1]
    up_pieces = ring(w_up, "y")
    sent_x, sent_c = prepare(tokens, cotangent)
    unit_x = jnp.concatenate(
        [sent_x[0]] + [shift(sent_x[k], "x", k) for k in range(1, 4)], axis=0
    )
    x_mine, x_other = over_dp(unit_x)
    down_pieces = [w_down] + [shift(w_down, "x", k) for k in range(1, 4)]
    unit_c = jnp.concatenate(
        [sent_c[0]] + [shift(sent_c[k], "y", k) for k in range(1, 4)], axis=0
    )
    c_mine, c_other = over_dp(unit_c)
    t_mine, t_other = over_dp(tokens)
    block = delta.astype(BF16)
    column = jnp.concatenate([block] + [shift(block, "y", k) for k in range(1, 4)], axis=0)
    blocks = [column] + [shift(column, "x", k) for k in range(1, 4)]
    terms, flipped = slot_terms(blk_row, blk_col, live, t_mine, t_other, blocks, width)

    partial = up_partial(x_mine, x_other, up_pieces)
    pre = total_of([partial[0]] + [shift(partial[k], "x", -k) for k in range(1, 4)]) + terms
    hidden = jax.nn.silu(pre).astype(BF16)
    partial = back_partial(c_mine, c_other, down_pieces)
    back = [partial[0]] + [shift(partial[k], "y", -k) for k in range(1, 4)]

    mine, other = out_partial(ring(hidden, "y"), down_pieces)
    chip = (mine.astype(F32) + swap_cores(other).astype(F32)).astype(BF16)
    line = total_of([chip[0]] + [shift(chip[k], "z", -k) for k in range(1, 4)]).astype(BF16)
    layer_out = finish([line[0]] + [shift(line[k], "y", -k) for k in range(1, 4)])

    factor = 1.0 / math.sqrt(4096.0)
    grads = slot_grads(blk_row, blk_col, live, pre, back, flipped, factor)
    row_sum = total_of([grads[0]] + [shift(grads[k], "x", k) for k in range(1, 4)])
    row_sum = row_sum.astype(BF16).reshape(4, 4, SIDE, SIDE)
    owned = total_of([row_sum[0]] + [shift(row_sum[k], "y", k) for k in range(1, 4)])
    new_first = 0.9 * first_moment + 0.1 * owned
    new_second = 0.95 * second_moment + 0.05 * owned * owned
    corrected_first = new_first / (1.0 - 0.9**10)
    corrected_second = new_second / (1.0 - 0.95**10)
    new_delta = delta - 0.01 * corrected_first / (jnp.sqrt(corrected_second) + 1e-08)
    return (layer_out, new_delta, new_first, new_second)


def solution(mesh):
    split = Mesh(mesh.devices.reshape(4, 2, 4, 4), DEVICE)
    return jax.shard_map(
        on_device,
        mesh=split,
        in_specs=(
            P(DEVICE, None),
            P(DEVICE, None),
            P(SHARD, DP),
            P(DP, SHARD),
            P(DEVICE, None, None),
            P(DEVICE, None, None),
            P(DEVICE, None, None),
            P(),
            P(),
            P(),
        ),
        out_specs=(
            P(DEVICE, None),
            P(DEVICE, None, None),
            P(DEVICE, None, None),
            P(DEVICE, None, None),
        ),
        check_vma=False,
    )
```

```python
import math

import jax
import jax.numpy as jnp
from jax import lax
from jax.experimental import pallas as pl
from jax.experimental.pallas import tpu as pltpu
from jax.sharding import Mesh
from jax.sharding import PartitionSpec as P


DEVICE = ("z", "c", "x", "y")
SHARD = ("x", "y")
DP = ("z", "c")
SIDE = 128
F32 = jnp.float32
BF16 = jnp.bfloat16


def shift(value, axis, by):
    return lax.ppermute(value, axis, [(k, (k + by) % 4) for k in range(4)])


def swap_cores(value):
    return lax.ppermute(value, "c", [(0, 1), (1, 0)])


def struct(shape, dtype):
    return jax.ShapeDtypeStruct(shape, dtype)


def cost(flops, nbytes):
    return pl.CostEstimate(flops=flops, bytes_accessed=nbytes, transcendentals=0)


def ring(piece, axis):
    half = piece.shape[0] // 2
    before = shift(piece, axis, 1)
    after = shift(piece, axis, -1)
    top = shift(before[:half], axis, 1)
    bottom = shift(after[half:], axis, -1)
    return piece, before, top, bottom, after


def ring_sum(parts, axis):
    own, before_a, before_b, top, bottom, after_a, after_b = parts
    top = shift(top, axis, -1)
    bottom = shift(bottom, axis, 1)
    before_b = shift(before_b, axis, -1)
    after_a = shift(after_a, axis, 1)
    before_a = shift(add(before_a, top), axis, -1)
    after_b = shift(add(after_b, bottom), axis, 1)
    return own, before_a, before_b, after_a, after_b


def add(a, b):
    return (a.astype(F32) + b.astype(F32)).astype(BF16)


def over_z(unit):
    pieces = {0: unit}
    for k in (1, 3, 2):
        pieces[k] = shift(unit, "z", k)
    return jnp.concatenate([pieces[k] for k in range(4)], axis=0)


def exchange(pieces, axis, sign):
    got = {0: pieces[0]}
    for k in (1, 3, 2):
        got[k] = shift(pieces[k], axis, sign * k)
    return [got[k] for k in range(4)]


def wrap(index):
    return lax.rem(index + 8, 4)


def prepare_kernel(tokens, cotangent, delta, t0, t1, t2, t3, c0, c1, c2, c3, chunks, block):
    x, y = lax.axis_index("x"), lax.axis_index("y")
    for k, out in enumerate((t0, t1, t2, t3)):
        out[...] = tokens[:, pl.ds(pl.multiple_of(wrap(x + k) * 1024, 1024), 1024)]
    for k, out in enumerate((c0, c1, c2, c3)):
        for i in range(4):
            begin = pl.multiple_of(i * 1024 + wrap(y + k) * 256, 256)
            out[:, i * 256 : (i + 1) * 256] = cotangent[:, pl.ds(begin, 256)]
    for q in range(4):
        chunks[q * 32 : (q + 1) * 32] = tokens[:, q * 1024 : (q + 1) * 1024]
    block[...] = delta[...].astype(BF16)


def prepare(tokens, cotangent, delta):
    outs = pl.pallas_call(
        prepare_kernel,
        out_shape=[struct((32, 1024), BF16)] * 8
        + [struct((128, 1024), BF16), struct(delta.shape, BF16)],
        cost_estimate=cost(0, 4 * tokens.size * 2),
    )(tokens, cotangent, delta)
    return outs[:4], outs[4:8], outs[8], outs[9]


def gather_rows(mine, other, lhs, position):
    stride = mine.shape[0] // 4
    for group in range(4):
        for core, ref in enumerate((mine, other)):
            for zr in range(4):
                to = group * 256 + core * 128 + zr * 32
                at = zr * stride + group * 32
                for k in range(4):
                    begin = pl.multiple_of(wrap(position - k) * 256, 256)
                    lhs[to : to + 32, k * 256 : (k + 1) * 256] = ref[
                        at : at + 32, pl.ds(begin, 256)
                    ]


def store_groups(lhs, rhs, dims, outs):
    at = 0
    total = None
    for out in outs:
        if at % 256 == 0:
            total = lax.dot_general(
                lhs[at : at + 256], rhs, (dims, ((), ())), preferred_element_type=F32
            )
        begin = at % 256
        out[...] = total[begin : begin + out.shape[0]].astype(BF16)
        at += out.shape[0]


def up_kernel(mine, other, w0, w1, w2a, w2b, w3, *rest):
    outs, lhs = rest[:-1], rest[-1]

    @pl.when(pl.program_id(0) == 0)
    def _():
        gather_rows(mine, other, lhs, lax.axis_index("y"))

    rhs = jnp.concatenate([w[...] for w in (w0, w1, w2a, w2b, w3)], axis=0)
    store_groups(lhs, rhs, ((1,), (0,)), outs)


GROUP_ROWS = (256,) + (128,) * 6
TILE = 896


def up_partial(mine, other, pieces):
    width = pieces[0].shape[1]
    whole = pl.BlockSpec(mine.shape, lambda n: (0, 0))
    return pl.pallas_call(
        up_kernel,
        grid=(width // TILE,),
        in_specs=[whole, whole]
        + [pl.BlockSpec((p.shape[0], TILE), lambda n: (0, n)) for p in pieces],
        out_specs=[pl.BlockSpec((256, TILE), lambda n: (0, n))] * 4,
        out_shape=[struct((256, width), BF16)] * 4,
        scratch_shapes=[pltpu.VMEM((1024, 1024), BF16)],
        cost_estimate=cost(2 * 1024 * 1024 * width, 4 * 1024 * width),
    )(mine, other, *pieces)


def back_kernel(mine, other, w0, w1, w2, w3, *rest):
    outs, lhs = rest[:-1], rest[-1]

    @pl.when(pl.program_id(0) == 0)
    def _():
        gather_rows(mine, other, lhs, lax.axis_index("x"))

    rhs = jnp.concatenate([w[...] for w in (w0, w1, w2, w3)], axis=1)
    store_groups(lhs, rhs, ((1,), (1,)), outs)


def back_partial(mine, other, pieces):
    width = pieces[0].shape[0]
    whole = pl.BlockSpec(mine.shape, lambda n: (0, 0))
    return pl.pallas_call(
        back_kernel,
        grid=(width // TILE,),
        in_specs=[whole, whole]
        + [pl.BlockSpec((TILE, 256), lambda n: (n, 0))] * 4,
        out_specs=[pl.BlockSpec((r, TILE), lambda n: (0, n)) for r in GROUP_ROWS],
        out_shape=[struct((r, width), BF16) for r in GROUP_ROWS],
        scratch_shapes=[pltpu.VMEM((1024, 1024), BF16)],
        cost_estimate=cost(2 * 1024 * 1024 * width, 4 * 1024 * width),
    )(mine, other, *pieces)


def pre_kernel(r0, r1, r2, r3, terms, pre, h_mine, h_other):
    n = pl.program_id(0)
    total = r0[...].astype(F32) + r1[...].astype(F32)
    total = total + r2[...].astype(F32) + (r3[...].astype(F32) + terms[...])
    pre[...] = total
    hidden = (total * jax.nn.sigmoid(total)).astype(BF16)

    @pl.when(n < 2)
    def _():
        h_mine[...] = hidden

    @pl.when(n >= 2)
    def _():
        h_other[...] = hidden


def pre_and_hidden(parts, terms):
    width = terms.shape[1]
    spec = pl.BlockSpec((64, width), lambda n: (n, 0))
    first = pl.BlockSpec((64, width), lambda n: (jnp.minimum(n, 1), 0))
    last = pl.BlockSpec((64, width), lambda n: (jnp.maximum(n - 2, 0), 0))
    return pl.pallas_call(
        pre_kernel,
        grid=(4,),
        in_specs=[spec] * 5,
        out_specs=[spec, first, last],
        out_shape=[
            struct((256, width), F32),
            struct((128, width), BF16),
            struct((128, width), BF16),
        ],
        cost_estimate=cost(0, 16 * 256 * width),
    )(*parts, terms)


def out_kernel(count, *refs):
    hidden, weights, rest = refs[:4], refs[4:8], refs[8:]
    lhs, outs = rest[-1], rest[count:-1]
    n = pl.program_id(0)

    @pl.when(n == 0)
    def _():
        at = 0
        for h in hidden:
            lhs[at : at + h.shape[0]] = h[...]
            at += h.shape[0]

    for pair in range(2):
        both = jnp.concatenate([weights[2 * pair][...], weights[2 * pair + 1][...]], axis=1)
        total = jnp.dot(lhs[...], both, preferred_element_type=F32)
        for half in range(2):
            at = pl.multiple_of((2 * pair + half) * 256 + n * 128, 128)
            for zr in range(4):
                for group in range(4):
                    row = group * 128 + zr * 32
                    term = total[row : row + 32, half * 128 : (half + 1) * 128]
                    if count:
                        term = term + rest[0][zr, group, :, pl.ds(at, 128)].astype(F32)
                    if count:
                        outs[zr][group, :, pl.ds(at, 128)] = term.astype(BF16)
                    else:
                        outs[0][zr, group, :, pl.ds(at, 128)] = term.astype(BF16)


def out_partial(hidden, pieces, theirs=()):
    width = pieces[0].shape[0]
    held = pl.BlockSpec((4, 4, 32, 1024), lambda n: (0, 0, 0, 0))
    part = pl.BlockSpec((4, 32, 1024), lambda n: (0, 0, 0))

    def kernel(*refs):
        out_kernel(len(theirs), *refs)

    return pl.pallas_call(
        kernel,
        grid=(2,),
        in_specs=[pl.BlockSpec(h.shape, lambda n: (0, 0)) for h in hidden]
        + [pl.BlockSpec((p.shape[0], 128), lambda n: (0, n)) for p in pieces]
        + [held] * len(theirs),
        out_specs=[part] * 4 if theirs else held,
        out_shape=[struct((4, 32, 1024), BF16)] * 4
        if theirs
        else struct((4, 4, 32, 1024), BF16),
        scratch_shapes=[pltpu.VMEM((512, width), BF16)],
        cost_estimate=cost(1024 * 1024 * width, 4 * 1024 * width),
    )(*hidden, *pieces, *theirs)


def slot_of(i, j, k, sign):
    x, y = lax.axis_index("x"), lax.axis_index("y")
    group = lax.axis_index("z") * 2 + lax.axis_index("c")
    return group * 64 + wrap(x + sign * i) * 16 + wrap(y + sign * j) * 4 + k


def place_of(slot, row, col, live):
    group = lax.axis_index("z") * 2 + lax.axis_index("c")
    at_row = pl.multiple_of(row[slot] * SIDE, SIDE)
    at_col = pl.multiple_of((col[slot] - group * 14) * SIDE, SIDE)
    return at_row, at_col, live[slot].astype(F32)


def terms_kernel(row, col, live, mine, other, b0, b1, b2, b3, terms, flipped, rows):
    terms[...] = jnp.zeros_like(terms)
    for core, ref in enumerate((mine, other)):
        for zr in range(4):
            for q in range(4):
                at = zr * 256 + 128 + q * 32
                to = core * 128 + zr * 32
                rows[to : to + 32, q * 1024 : (q + 1) * 1024] = ref[at : at + 32]
    for j, ref in enumerate((b0, b1, b2, b3)):
        for i in range(4):
            for k in range(4):
                at_row, at_col, flag = place_of(slot_of(i, j, k, -1), row, col, live)
                term = jnp.dot(
                    rows[:, pl.ds(at_row, SIDE)], ref[i * 4 + k], preferred_element_type=F32
                )
                here = (slice(None), pl.ds(at_col, SIDE))
                terms[here] = terms[here] + term * flag
    for r in range(32):
        flipped[r * 128 : (r + 1) * 128] = rows[:, r * 128 : (r + 1) * 128].T


def slot_terms(row, col, live, mine, other, blocks, width):
    smem = pl.BlockSpec(memory_space=pltpu.SMEM)
    vmem = pl.BlockSpec(memory_space=pltpu.VMEM)
    return pl.pallas_call(
        terms_kernel,
        in_specs=[smem] * 3 + [vmem] * 6,
        out_specs=[vmem, vmem],
        out_shape=[struct((256, width), F32), struct((4096, 256), BF16)],
        scratch_shapes=[pltpu.VMEM((256, 4096), BF16)],
        cost_estimate=cost(64 * 2 * 256 * 128 * 128, 8 << 20),
    )(row, col, live, mine, other, *blocks)


def grads_kernel(factor, row, col, live, pre, own, a1, b1, a3, b3, flipped, g0, g1, g2, g3, dpre):
    for core, (r1, r3) in enumerate(((a1, a3), (b1, b3))):
        rows = slice(core * 128, (core + 1) * 128)
        for n in range(pre.shape[1] // 256):
            at = slice(n * 256, (n + 1) * 256)
            back = own[rows, at].astype(F32) + r1[:, at].astype(F32)
            back = back + r3[:, at].astype(F32)
            value = pre[rows, at]
            sigma = jax.nn.sigmoid(value)
            dpre[rows, at] = (back * sigma * (1.0 + value * (1.0 - sigma))).astype(BF16)
    for i, out in enumerate((g0, g1, g2, g3)):
        for j in range(4):
            for k in range(4):
                at_row, at_col, flag = place_of(slot_of(i, j, k, 1), row, col, live)
                grad = jnp.dot(
                    flipped[pl.ds(at_row, SIDE), :],
                    dpre[:, pl.ds(at_col, SIDE)],
                    preferred_element_type=F32,
                )
                out[j * 4 + k] = (grad * (flag * factor)).astype(BF16)


def slot_grads(row, col, live, pre, back, flipped, factor):
    smem = pl.BlockSpec(memory_space=pltpu.SMEM)
    vmem = pl.BlockSpec(memory_space=pltpu.VMEM)

    def kernel(*refs):
        grads_kernel(factor, *refs)

    return pl.pallas_call(
        kernel,
        in_specs=[smem] * 3 + [vmem] * 7,
        out_specs=[vmem] * 4,
        out_shape=[struct((16, SIDE, SIDE), BF16)] * 4,
        scratch_shapes=[pltpu.VMEM(back[0].shape, BF16)],
        cost_estimate=cost(64 * 2 * 256 * 128 * 128, 8 << 20),
    )(row, col, live, pre, *back, flipped)


def finish_kernel(r0, r1, r2, r3, out):
    x, y = lax.axis_index("x"), lax.axis_index("y")
    for j, ref in enumerate((r0, r1, r2, r3)):
        for i in range(4):
            begin = pl.multiple_of(wrap(x - i) * 1024 + wrap(y + j) * 256, 256)
            out[:, pl.ds(begin, 256)] = ref[:, i * 256 : (i + 1) * 256]


def finish(pieces):
    return pl.pallas_call(
        finish_kernel,
        out_shape=struct((32, 4096), BF16),
        cost_estimate=cost(0, 1 << 19),
    )(*pieces)


def total_of(pieces):
    total = pieces[0].astype(F32)
    for piece in pieces[1:]:
        total = total + piece.astype(F32)
    return total


def on_device(
    tokens, cotangent, w_up, w_down, delta, first_moment, second_moment, blk_row, blk_col, live
):
    width = w_up.shape[1]
    up_pieces = ring(w_up, "y")
    sent_x, sent_c, chunks, block = prepare(tokens, cotangent, delta)
    unit = jnp.concatenate(exchange(sent_x, "x", 1), axis=0)
    x_mine = over_z(unit)
    x_other = swap_cores(x_mine)
    down_pieces = exchange([w_down] * 4, "x", 1)
    unit = jnp.concatenate(exchange(sent_c, "y", 1) + [chunks], axis=0)
    t_mine = over_z(unit)
    t_other = swap_cores(t_mine)
    column = exchange([block] * 4, "x", 1)
    column = jnp.concatenate(column, axis=0)
    blocks = exchange([column] * 4, "y", 1)
    terms, flipped = slot_terms(blk_row, blk_col, live, t_mine, t_other, blocks, width)

    pre_parts = exchange(up_partial(x_mine, x_other, up_pieces), "x", -1)
    pre, h_mine, h_other = pre_and_hidden(pre_parts, terms)
    back = ring_sum(back_partial(t_mine, t_other, down_pieces), "y")

    a1, a3 = shift(h_other, "y", 1), shift(h_other, "y", -1)
    b1, b3 = shift(h_mine, "y", 1), shift(h_mine, "y", -1)
    a2, b2 = shift(a3, "y", -1), shift(b1, "y", 1)
    theirs = out_partial([h_other, a1, a2, a3], down_pieces)
    theirs = swap_cores(theirs)
    chip = out_partial([h_mine, b1, b2, b3], down_pieces, (theirs,))
    line = total_of(exchange(chip, "z", -1)).astype(BF16)
    layer_out = finish(exchange([line[k] for k in range(4)], "y", -1))

    factor = 1.0 / math.sqrt(4096.0)
    grads = slot_grads(blk_row, blk_col, live, pre, back, flipped, factor)
    row_sum = total_of(exchange(grads, "x", 1)).astype(BF16).reshape(4, 4, SIDE, SIDE)
    owned = total_of(exchange([row_sum[k] for k in range(4)], "y", 1))
    new_first = 0.9 * first_moment + 0.1 * owned
    new_second = 0.95 * second_moment + 0.05 * owned * owned
    corrected_first = new_first / (1.0 - 0.9**10)
    corrected_second = new_second / (1.0 - 0.95**10)
    new_delta = delta - 0.01 * corrected_first / (jnp.sqrt(corrected_second) + 1e-08)
    return (layer_out, new_delta, new_first, new_second)


def solution(mesh):
    split = Mesh(mesh.devices.reshape(4, 2, 4, 4), DEVICE)
    return jax.shard_map(
        on_device,
        mesh=split,
        in_specs=(
            P(DEVICE, None),
            P(DEVICE, None),
            P(SHARD, DP),
            P(DP, SHARD),
            P(DEVICE, None, None),
            P(DEVICE, None, None),
            P(DEVICE, None, None),
            P(),
            P(),
            P(),
        ),
        out_specs=(
            P(DEVICE, None),
            P(DEVICE, None, None),
            P(DEVICE, None, None),
            P(DEVICE, None, None),
        ),
        check_vma=False,
    )
```

```python
import math

import jax
import jax.numpy as jnp
from jax import lax
from jax.experimental import pallas as pl
from jax.experimental.pallas import tpu as pltpu
from jax.sharding import Mesh
from jax.sharding import PartitionSpec as P


DEVICE = ("z", "c", "x", "y")
SHARD = ("x", "y")
DP = ("z", "c")
SIDE = 128
F32 = jnp.float32
BF16 = jnp.bfloat16


def shift(value, axis, by):
    return lax.ppermute(value, axis, [(k, (k + by) % 4) for k in range(4)])


def swap_cores(value):
    return lax.ppermute(value, "c", [(0, 1), (1, 0)])


def struct(shape, dtype):
    return jax.ShapeDtypeStruct(shape, dtype)


def cost(flops, nbytes):
    return pl.CostEstimate(flops=flops, bytes_accessed=nbytes, transcendentals=0)


def ring(piece, axis):
    half = piece.shape[0] // 2
    before = shift(piece, axis, 1)
    after = shift(piece, axis, -1)
    top = shift(before[:half], axis, 1)
    bottom = shift(after[half:], axis, -1)
    return piece, before, top, bottom, after


def ring_sum(parts, axis):
    own, before_a, before_b, top, bottom, after_a, after_b = parts
    top = shift(top, axis, -1)
    bottom = shift(bottom, axis, 1)
    before_b = shift(before_b, axis, -1)
    after_a = shift(after_a, axis, 1)
    before_a = shift(add(before_a, top), axis, -1)
    after_b = shift(add(after_b, bottom), axis, 1)
    return own, before_a, before_b, after_a, after_b


def add(a, b):
    return (a.astype(F32) + b.astype(F32)).astype(BF16)


def over_z(unit):
    pieces = {0: unit}
    for k in (1, 3, 2):
        pieces[k] = shift(unit, "z", k)
    return jnp.concatenate([pieces[k] for k in range(4)], axis=0)


def exchange(pieces, axis, sign):
    got = {0: pieces[0]}
    for k in (1, 3, 2):
        got[k] = shift(pieces[k], axis, sign * k)
    return [got[k] for k in range(4)]


def wrap(index):
    return lax.rem(index + 8, 4)


def prepare_kernel(tokens, cotangent, delta, t0, t1, t2, t3, c0, c1, c2, c3, chunks, block):
    x, y = lax.axis_index("x"), lax.axis_index("y")
    for k, out in enumerate((t0, t1, t2, t3)):
        out[...] = tokens[:, pl.ds(pl.multiple_of(wrap(x + k) * 1024, 1024), 1024)]
    for k, out in enumerate((c0, c1, c2, c3)):
        for i in range(4):
            begin = pl.multiple_of(i * 1024 + wrap(y + k) * 256, 256)
            out[:, i * 256 : (i + 1) * 256] = cotangent[:, pl.ds(begin, 256)]
    for q in range(4):
        chunks[q * 32 : (q + 1) * 32] = tokens[:, q * 1024 : (q + 1) * 1024]
    block[...] = delta[...].astype(BF16)


def prepare(tokens, cotangent, delta):
    outs = pl.pallas_call(
        prepare_kernel,
        out_shape=[struct((32, 1024), BF16)] * 8
        + [struct((128, 1024), BF16), struct(delta.shape, BF16)],
        cost_estimate=cost(0, 4 * tokens.size * 2),
    )(tokens, cotangent, delta)
    return outs[:4], outs[4:8], outs[8], outs[9]


def gather_rows(mine, other, lhs, position):
    stride = mine.shape[0] // 4
    for group in range(4):
        for core, ref in enumerate((mine, other)):
            for zr in range(4):
                to = group * 256 + core * 128 + zr * 32
                at = zr * stride + group * 32
                for k in range(4):
                    begin = pl.multiple_of(wrap(position - k) * 256, 256)
                    lhs[to : to + 32, k * 256 : (k + 1) * 256] = ref[
                        at : at + 32, pl.ds(begin, 256)
                    ]


def store_groups(lhs, rhs, dims, outs):
    at = 0
    total = None
    for out in outs:
        if at % 256 == 0:
            total = lax.dot_general(
                lhs[at : at + 256], rhs, (dims, ((), ())), preferred_element_type=F32
            )
        begin = at % 256
        out[...] = total[begin : begin + out.shape[0]].astype(BF16)
        at += out.shape[0]


def up_kernel(mine, other, w0, w1, w2a, w2b, w3, *rest):
    outs, lhs = rest[:-1], rest[-1]

    @pl.when(pl.program_id(0) == 0)
    def _():
        gather_rows(mine, other, lhs, lax.axis_index("y"))

    rhs = jnp.concatenate([w[...] for w in (w0, w1, w2a, w2b, w3)], axis=0)
    store_groups(lhs, rhs, ((1,), (0,)), outs)


GROUP_ROWS = (256,) + (128,) * 6
TILE = 896


def up_partial(mine, other, pieces):
    width = pieces[0].shape[1]
    whole = pl.BlockSpec(mine.shape, lambda n: (0, 0))
    return pl.pallas_call(
        up_kernel,
        grid=(width // TILE,),
        in_specs=[whole, whole]
        + [pl.BlockSpec((p.shape[0], TILE), lambda n: (0, n)) for p in pieces],
        out_specs=[pl.BlockSpec((r, TILE), lambda n: (0, n)) for r in GROUP_ROWS],
        out_shape=[struct((r, width), BF16) for r in GROUP_ROWS],
        scratch_shapes=[pltpu.VMEM((1024, 1024), BF16)],
        cost_estimate=cost(2 * 1024 * 1024 * width, 4 * 1024 * width),
    )(mine, other, *pieces)


def back_kernel(mine, other, w0, w1, w2, w3, *rest):
    outs, lhs = rest[:-1], rest[-1]

    @pl.when(pl.program_id(0) == 0)
    def _():
        gather_rows(mine, other, lhs, lax.axis_index("x"))

    rhs = jnp.concatenate([w[...] for w in (w0, w1, w2, w3)], axis=1)
    store_groups(lhs, rhs, ((1,), (1,)), outs)


def back_partial(mine, other, pieces):
    width = pieces[0].shape[0]
    whole = pl.BlockSpec(mine.shape, lambda n: (0, 0))
    return pl.pallas_call(
        back_kernel,
        grid=(width // TILE,),
        in_specs=[whole, whole]
        + [pl.BlockSpec((TILE, 256), lambda n: (n, 0))] * 4,
        out_specs=[pl.BlockSpec((r, TILE), lambda n: (0, n)) for r in GROUP_ROWS],
        out_shape=[struct((r, width), BF16) for r in GROUP_ROWS],
        scratch_shapes=[pltpu.VMEM((1024, 1024), BF16)],
        cost_estimate=cost(2 * 1024 * 1024 * width, 4 * 1024 * width),
    )(mine, other, *pieces)


def pre_kernel(own, a1, b1, a3, b3, terms, pre, h_mine, h_other):
    n = pl.program_id(0)
    r1 = jnp.where(n < 2, a1[...], b1[...]).astype(F32)
    r3 = jnp.where(n < 2, a3[...], b3[...]).astype(F32)
    total = own[...].astype(F32) + r1 + (r3 + terms[...])
    pre[...] = total
    hidden = (total * jax.nn.sigmoid(total)).astype(BF16)

    @pl.when(n < 2)
    def _():
        h_mine[...] = hidden

    @pl.when(n >= 2)
    def _():
        h_other[...] = hidden


def pre_and_hidden(parts, terms):
    width = terms.shape[1]
    spec = pl.BlockSpec((64, width), lambda n: (n, 0))
    first = pl.BlockSpec((64, width), lambda n: (jnp.minimum(n, 1), 0))
    last = pl.BlockSpec((64, width), lambda n: (jnp.maximum(n - 2, 0), 0))
    return pl.pallas_call(
        pre_kernel,
        grid=(4,),
        in_specs=[spec, first, last, first, last, spec],
        out_specs=[spec, first, last],
        out_shape=[
            struct((256, width), F32),
            struct((128, width), BF16),
            struct((128, width), BF16),
        ],
        cost_estimate=cost(0, 16 * 256 * width),
    )(*parts, terms)


def out_kernel(count, *refs):
    hidden, weights, rest = refs[:4], refs[4:8], refs[8:]
    lhs, outs = rest[-1], rest[count:-1]
    n = pl.program_id(0)

    @pl.when(n == 0)
    def _():
        at = 0
        for h in hidden:
            lhs[at : at + h.shape[0]] = h[...]
            at += h.shape[0]

    for pair in range(2):
        both = jnp.concatenate([weights[2 * pair][...], weights[2 * pair + 1][...]], axis=1)
        total = jnp.dot(lhs[...], both, preferred_element_type=F32)
        for half in range(2):
            at = pl.multiple_of((2 * pair + half) * 256 + n * 128, 128)
            for zr in range(4):
                for group in range(4):
                    row = group * 128 + zr * 32
                    term = total[row : row + 32, half * 128 : (half + 1) * 128]
                    if count:
                        term = term + rest[0][zr, group, :, pl.ds(at, 128)].astype(F32)
                    if count:
                        outs[zr][group, :, pl.ds(at, 128)] = term.astype(BF16)
                    else:
                        outs[0][zr, group, :, pl.ds(at, 128)] = term.astype(BF16)


def out_partial(hidden, pieces, theirs=()):
    width = pieces[0].shape[0]
    held = pl.BlockSpec((4, 4, 32, 1024), lambda n: (0, 0, 0, 0))
    part = pl.BlockSpec((4, 32, 1024), lambda n: (0, 0, 0))

    def kernel(*refs):
        out_kernel(len(theirs), *refs)

    return pl.pallas_call(
        kernel,
        grid=(2,),
        in_specs=[pl.BlockSpec(h.shape, lambda n: (0, 0)) for h in hidden]
        + [pl.BlockSpec((p.shape[0], 128), lambda n: (0, n)) for p in pieces]
        + [held] * len(theirs),
        out_specs=[part] * 4 if theirs else held,
        out_shape=[struct((4, 32, 1024), BF16)] * 4
        if theirs
        else struct((4, 4, 32, 1024), BF16),
        scratch_shapes=[pltpu.VMEM((512, width), BF16)],
        cost_estimate=cost(1024 * 1024 * width, 4 * 1024 * width),
    )(*hidden, *pieces, *theirs)


def slot_of(i, j, k, sign):
    x, y = lax.axis_index("x"), lax.axis_index("y")
    group = lax.axis_index("z") * 2 + lax.axis_index("c")
    return group * 64 + wrap(x + sign * i) * 16 + wrap(y + sign * j) * 4 + k


def place_of(slot, row, col, live):
    group = lax.axis_index("z") * 2 + lax.axis_index("c")
    at_row = pl.multiple_of(row[slot] * SIDE, SIDE)
    at_col = pl.multiple_of((col[slot] - group * 14) * SIDE, SIDE)
    return at_row, at_col, live[slot].astype(F32)


def terms_kernel(row, col, live, mine, other, b0, b1, b2, b3, terms, flipped, rows):
    terms[...] = jnp.zeros_like(terms)
    for core, ref in enumerate((mine, other)):
        for zr in range(4):
            for q in range(4):
                at = zr * 256 + 128 + q * 32
                to = core * 128 + zr * 32
                rows[to : to + 32, q * 1024 : (q + 1) * 1024] = ref[at : at + 32]
    for j, ref in enumerate((b0, b1, b2, b3)):
        for i in range(4):
            for k in range(4):
                at_row, at_col, flag = place_of(slot_of(i, j, k, -1), row, col, live)
                term = jnp.dot(
                    rows[:, pl.ds(at_row, SIDE)], ref[i * 4 + k], preferred_element_type=F32
                )
                here = (slice(None), pl.ds(at_col, SIDE))
                terms[here] = terms[here] + term * flag
    for r in range(32):
        flipped[r * 128 : (r + 1) * 128] = rows[:, r * 128 : (r + 1) * 128].T


def slot_terms(row, col, live, mine, other, blocks, width):
    smem = pl.BlockSpec(memory_space=pltpu.SMEM)
    vmem = pl.BlockSpec(memory_space=pltpu.VMEM)
    return pl.pallas_call(
        terms_kernel,
        in_specs=[smem] * 3 + [vmem] * 6,
        out_specs=[vmem, vmem],
        out_shape=[struct((256, width), F32), struct((4096, 256), BF16)],
        scratch_shapes=[pltpu.VMEM((256, 4096), BF16)],
        cost_estimate=cost(64 * 2 * 256 * 128 * 128, 8 << 20),
    )(row, col, live, mine, other, *blocks)


def grads_kernel(factor, row, col, live, pre, own, a1, b1, a3, b3, flipped, g0, g1, g2, g3, dpre):
    for core, (r1, r3) in enumerate(((a1, a3), (b1, b3))):
        rows = slice(core * 128, (core + 1) * 128)
        for n in range(pre.shape[1] // 256):
            at = slice(n * 256, (n + 1) * 256)
            back = own[rows, at].astype(F32) + r1[:, at].astype(F32)
            back = back + r3[:, at].astype(F32)
            value = pre[rows, at]
            sigma = jax.nn.sigmoid(value)
            dpre[rows, at] = (back * sigma * (1.0 + value * (1.0 - sigma))).astype(BF16)
    for i, out in enumerate((g0, g1, g2, g3)):
        for j in range(4):
            for k in range(4):
                at_row, at_col, flag = place_of(slot_of(i, j, k, 1), row, col, live)
                grad = jnp.dot(
                    flipped[pl.ds(at_row, SIDE), :],
                    dpre[:, pl.ds(at_col, SIDE)],
                    preferred_element_type=F32,
                )
                out[j * 4 + k] = (grad * (flag * factor)).astype(BF16)


def slot_grads(row, col, live, pre, back, flipped, factor):
    smem = pl.BlockSpec(memory_space=pltpu.SMEM)
    vmem = pl.BlockSpec(memory_space=pltpu.VMEM)

    def kernel(*refs):
        grads_kernel(factor, *refs)

    return pl.pallas_call(
        kernel,
        in_specs=[smem] * 3 + [vmem] * 7,
        out_specs=[vmem] * 4,
        out_shape=[struct((16, SIDE, SIDE), BF16)] * 4,
        scratch_shapes=[pltpu.VMEM(back[0].shape, BF16)],
        cost_estimate=cost(64 * 2 * 256 * 128 * 128, 8 << 20),
    )(row, col, live, pre, *back, flipped)


def finish_kernel(r0, r1, r2, r3, out):
    x, y = lax.axis_index("x"), lax.axis_index("y")
    for j, ref in enumerate((r0, r1, r2, r3)):
        for i in range(4):
            begin = pl.multiple_of(wrap(x - i) * 1024 + wrap(y + j) * 256, 256)
            out[:, pl.ds(begin, 256)] = ref[:, i * 256 : (i + 1) * 256]


def finish(pieces):
    return pl.pallas_call(
        finish_kernel,
        out_shape=struct((32, 4096), BF16),
        cost_estimate=cost(0, 1 << 19),
    )(*pieces)


def total_of(pieces):
    total = pieces[0].astype(F32)
    for piece in pieces[1:]:
        total = total + piece.astype(F32)
    return total


def on_device(
    tokens, cotangent, w_up, w_down, delta, first_moment, second_moment, blk_row, blk_col, live
):
    width = w_up.shape[1]
    up_pieces = ring(w_up, "y")
    sent_x, sent_c, chunks, block = prepare(tokens, cotangent, delta)
    unit = jnp.concatenate(exchange(sent_x, "x", 1), axis=0)
    x_mine = over_z(unit)
    x_other = swap_cores(x_mine)
    down_pieces = exchange([w_down] * 4, "x", 1)
    unit = jnp.concatenate(exchange(sent_c, "y", 1) + [chunks], axis=0)
    t_mine = over_z(unit)
    t_other = swap_cores(t_mine)
    column = exchange([block] * 4, "x", 1)
    column = jnp.concatenate(column, axis=0)
    blocks = exchange([column] * 4, "y", 1)
    terms, flipped = slot_terms(blk_row, blk_col, live, t_mine, t_other, blocks, width)

    pre_parts = ring_sum(up_partial(x_mine, x_other, up_pieces), "x")
    pre, h_mine, h_other = pre_and_hidden(pre_parts, terms)
    back = ring_sum(back_partial(t_mine, t_other, down_pieces), "y")

    a1, a3 = shift(h_other, "y", 1), shift(h_other, "y", -1)
    b1, b3 = shift(h_mine, "y", 1), shift(h_mine, "y", -1)
    a2, b2 = shift(a3, "y", -1), shift(b1, "y", 1)
    theirs = out_partial([h_other, a1, a2, a3], down_pieces)
    theirs = swap_cores(theirs)
    chip = out_partial([h_mine, b1, b2, b3], down_pieces, (theirs,))
    line = total_of(exchange(chip, "z", -1)).astype(BF16)
    layer_out = finish(exchange([line[k] for k in range(4)], "y", -1))

    factor = 1.0 / math.sqrt(4096.0)
    grads = slot_grads(blk_row, blk_col, live, pre, back, flipped, factor)
    row_sum = total_of(exchange(grads, "x", 1)).astype(BF16).reshape(4, 4, SIDE, SIDE)
    owned = total_of(exchange([row_sum[k] for k in range(4)], "y", 1))
    new_first = 0.9 * first_moment + 0.1 * owned
    new_second = 0.95 * second_moment + 0.05 * owned * owned
    corrected_first = new_first / (1.0 - 0.9**10)
    corrected_second = new_second / (1.0 - 0.95**10)
    new_delta = delta - 0.01 * corrected_first / (jnp.sqrt(corrected_second) + 1e-08)
    return (layer_out, new_delta, new_first, new_second)


def solution(mesh):
    split = Mesh(mesh.devices.reshape(4, 2, 4, 4), DEVICE)
    return jax.shard_map(
        on_device,
        mesh=split,
        in_specs=(
            P(DEVICE, None),
            P(DEVICE, None),
            P(SHARD, DP),
            P(DP, SHARD),
            P(DEVICE, None, None),
            P(DEVICE, None, None),
            P(DEVICE, None, None),
            P(),
            P(),
            P(),
        ),
        out_specs=(
            P(DEVICE, None),
            P(DEVICE, None, None),
            P(DEVICE, None, None),
            P(DEVICE, None, None),
        ),
        check_vma=False,
    )
```

```python
import math

import jax
import jax.numpy as jnp
from jax import lax
from jax.experimental import pallas as pl
from jax.experimental.pallas import tpu as pltpu
from jax.sharding import Mesh
from jax.sharding import PartitionSpec as P


DEVICE = ("z", "c", "x", "y")
SHARD = ("x", "y")
DP = ("z", "c")
SIDE = 128
F32 = jnp.float32
BF16 = jnp.bfloat16


def shift(value, axis, by):
    return lax.ppermute(value, axis, [(k, (k + by) % 4) for k in range(4)])


def swap_cores(value):
    return lax.ppermute(value, "c", [(0, 1), (1, 0)])


def struct(shape, dtype):
    return jax.ShapeDtypeStruct(shape, dtype)


def cost(flops, nbytes):
    return pl.CostEstimate(flops=flops, bytes_accessed=nbytes, transcendentals=0)


def ring(piece, axis):
    half = piece.shape[0] // 2
    before = shift(piece, axis, 1)
    after = shift(piece, axis, -1)
    top = shift(before[:half], axis, 1)
    bottom = shift(after[half:], axis, -1)
    return piece, before, top, bottom, after


def ring_sum(parts, axis):
    own, before_a, before_b, top, bottom, after_a, after_b = parts
    top = shift(top, axis, -1)
    bottom = shift(bottom, axis, 1)
    before_b = shift(before_b, axis, -1)
    after_a = shift(after_a, axis, 1)
    before_a = shift(add(before_a, top), axis, -1)
    after_b = shift(add(after_b, bottom), axis, 1)
    return own, before_a, before_b, after_a, after_b


def add(a, b):
    return (a.astype(F32) + b.astype(F32)).astype(BF16)


def over_z(unit):
    pieces = {0: unit}
    for k in (1, 3, 2):
        pieces[k] = shift(unit, "z", k)
    return jnp.concatenate([pieces[k] for k in range(4)], axis=0)


def exchange(pieces, axis, sign):
    got = {0: pieces[0]}
    for k in (1, 3, 2):
        got[k] = shift(pieces[k], axis, sign * k)
    return [got[k] for k in range(4)]


def wrap(index):
    return lax.rem(index + 8, 4)


def prepare_kernel(tokens, cotangent, delta, t0, t1, t2, t3, c0, c1, c2, c3, chunks, block):
    x, y = lax.axis_index("x"), lax.axis_index("y")
    for k, out in enumerate((t0, t1, t2, t3)):
        out[...] = tokens[:, pl.ds(pl.multiple_of(wrap(x + k) * 1024, 1024), 1024)]
    for k, out in enumerate((c0, c1, c2, c3)):
        for i in range(4):
            begin = pl.multiple_of(i * 1024 + wrap(y + k) * 256, 256)
            out[:, i * 256 : (i + 1) * 256] = cotangent[:, pl.ds(begin, 256)]
    for q in range(4):
        chunks[q * 32 : (q + 1) * 32] = tokens[:, q * 1024 : (q + 1) * 1024]
    block[...] = delta[...].astype(BF16)


def prepare(tokens, cotangent, delta):
    outs = pl.pallas_call(
        prepare_kernel,
        out_shape=[struct((32, 1024), BF16)] * 8
        + [struct((128, 1024), BF16), struct(delta.shape, BF16)],
        cost_estimate=cost(0, 4 * tokens.size * 2),
    )(tokens, cotangent, delta)
    return outs[:4], outs[4:8], outs[8], outs[9]


def gather_rows(mine, other, lhs, position):
    stride = mine.shape[0] // 4
    for group in range(4):
        for core, ref in enumerate((mine, other)):
            for zr in range(4):
                to = group * 256 + core * 128 + zr * 32
                at = zr * stride + group * 32
                for k in range(4):
                    begin = pl.multiple_of(wrap(position - k) * 256, 256)
                    lhs[to : to + 32, k * 256 : (k + 1) * 256] = ref[
                        at : at + 32, pl.ds(begin, 256)
                    ]


def store_groups(lhs, rhs, dims, outs):
    at = 0
    total = None
    for out in outs:
        if at % 256 == 0:
            total = lax.dot_general(
                lhs[at : at + 256], rhs, (dims, ((), ())), preferred_element_type=F32
            )
        begin = at % 256
        out[...] = total[begin : begin + out.shape[0]].astype(BF16)
        at += out.shape[0]


def up_kernel(mine, other, w0, w1, w2a, w2b, w3, *rest):
    outs, lhs = rest[:-1], rest[-1]

    @pl.when(pl.program_id(0) == 0)
    def _():
        gather_rows(mine, other, lhs, lax.axis_index("y"))

    rhs = jnp.concatenate([w[...] for w in (w0, w1, w2a, w2b, w3)], axis=0)
    store_groups(lhs, rhs, ((1,), (0,)), outs)


GROUP_ROWS = (256,) + (128,) * 6
TILE = 896


def up_partial(mine, other, pieces):
    width = pieces[0].shape[1]
    whole = pl.BlockSpec(mine.shape, lambda n: (0, 0))
    return pl.pallas_call(
        up_kernel,
        grid=(width // TILE,),
        in_specs=[whole, whole]
        + [pl.BlockSpec((p.shape[0], TILE), lambda n: (0, n)) for p in pieces],
        out_specs=[pl.BlockSpec((r, TILE), lambda n: (0, n)) for r in GROUP_ROWS],
        out_shape=[struct((r, width), BF16) for r in GROUP_ROWS],
        scratch_shapes=[pltpu.VMEM((1024, 1024), BF16)],
        cost_estimate=cost(2 * 1024 * 1024 * width, 4 * 1024 * width),
    )(mine, other, *pieces)


def back_kernel(mine, other, w0, w1, w2, w3, *rest):
    outs, lhs = rest[:-1], rest[-1]

    @pl.when(pl.program_id(0) == 0)
    def _():
        gather_rows(mine, other, lhs, lax.axis_index("x"))

    rhs = jnp.concatenate([w[...] for w in (w0, w1, w2, w3)], axis=1)
    store_groups(lhs, rhs, ((1,), (1,)), outs)


def back_partial(mine, other, pieces):
    width = pieces[0].shape[0]
    whole = pl.BlockSpec(mine.shape, lambda n: (0, 0))
    return pl.pallas_call(
        back_kernel,
        grid=(width // TILE,),
        in_specs=[whole, whole]
        + [pl.BlockSpec((TILE, 256), lambda n: (n, 0))] * 4,
        out_specs=[pl.BlockSpec((r, TILE), lambda n: (0, n)) for r in GROUP_ROWS],
        out_shape=[struct((r, width), BF16) for r in GROUP_ROWS],
        scratch_shapes=[pltpu.VMEM((1024, 1024), BF16)],
        cost_estimate=cost(2 * 1024 * 1024 * width, 4 * 1024 * width),
    )(mine, other, *pieces)


def pre_kernel(own, a1, b1, a3, b3, terms, pre, h_mine, h_other):
    n = pl.program_id(0)
    r1 = jnp.where(n < 2, a1[...], b1[...]).astype(F32)
    r3 = jnp.where(n < 2, a3[...], b3[...]).astype(F32)
    total = own[...].astype(F32) + r1 + (r3 + terms[...])
    pre[...] = total
    hidden = (total * jax.nn.sigmoid(total)).astype(BF16)

    @pl.when(n < 2)
    def _():
        h_mine[...] = hidden

    @pl.when(n >= 2)
    def _():
        h_other[...] = hidden


def pre_and_hidden(parts, terms):
    width = terms.shape[1]
    spec = pl.BlockSpec((64, width), lambda n: (n, 0))
    first = pl.BlockSpec((64, width), lambda n: (jnp.minimum(n, 1), 0))
    last = pl.BlockSpec((64, width), lambda n: (jnp.maximum(n - 2, 0), 0))
    return pl.pallas_call(
        pre_kernel,
        grid=(4,),
        in_specs=[spec, first, last, first, last, spec],
        out_specs=[spec, first, last],
        out_shape=[
            struct((256, width), F32),
            struct((128, width), BF16),
            struct((128, width), BF16),
        ],
        cost_estimate=cost(0, 16 * 256 * width),
    )(*parts, terms)


def out_kernel(count, *refs):
    hidden, weights, rest = refs[:4], refs[4:8], refs[8:]
    lhs, outs = rest[-1], rest[count:-1]
    n = pl.program_id(0)

    @pl.when(n == 0)
    def _():
        at = 0
        for h in hidden:
            lhs[at : at + h.shape[0]] = h[...]
            at += h.shape[0]

    for pair in range(2):
        both = jnp.concatenate([weights[2 * pair][...], weights[2 * pair + 1][...]], axis=1)
        total = jnp.dot(lhs[...], both, preferred_element_type=F32)
        for half in range(2):
            at = pl.multiple_of((2 * pair + half) * 256 + n * 128, 128)
            for zr in range(4):
                for group in range(4):
                    row = group * 128 + zr * 32
                    term = total[row : row + 32, half * 128 : (half + 1) * 128]
                    if count:
                        term = term + rest[0][zr, group, :, pl.ds(at, 128)].astype(F32)
                    if count:
                        outs[zr][group, :, pl.ds(at, 128)] = term.astype(BF16)
                    else:
                        outs[0][zr, group, :, pl.ds(at, 128)] = term.astype(BF16)


def out_partial(hidden, pieces, theirs=()):
    width = pieces[0].shape[0]
    held = pl.BlockSpec((4, 4, 32, 1024), lambda n: (0, 0, 0, 0))
    part = pl.BlockSpec((4, 32, 1024), lambda n: (0, 0, 0))

    def kernel(*refs):
        out_kernel(len(theirs), *refs)

    return pl.pallas_call(
        kernel,
        grid=(2,),
        in_specs=[pl.BlockSpec(h.shape, lambda n: (0, 0)) for h in hidden]
        + [pl.BlockSpec((p.shape[0], 128), lambda n: (0, n)) for p in pieces]
        + [held] * len(theirs),
        out_specs=[part] * 4 if theirs else held,
        out_shape=[struct((4, 32, 1024), BF16)] * 4
        if theirs
        else struct((4, 4, 32, 1024), BF16),
        scratch_shapes=[pltpu.VMEM((512, width), BF16)],
        cost_estimate=cost(1024 * 1024 * width, 4 * 1024 * width),
    )(*hidden, *pieces, *theirs)


def slot_of(i, j, k, sign):
    x, y = lax.axis_index("x"), lax.axis_index("y")
    group = lax.axis_index("z") * 2 + lax.axis_index("c")
    return group * 64 + wrap(x + sign * i) * 16 + wrap(y + sign * j) * 4 + k


def place_of(slot, row, col, live):
    group = lax.axis_index("z") * 2 + lax.axis_index("c")
    at_row = pl.multiple_of(row[slot] * SIDE, SIDE)
    at_col = pl.multiple_of((col[slot] - group * 14) * SIDE, SIDE)
    return at_row, at_col, live[slot].astype(F32)


def terms_kernel(row, col, live, mine, other, b0, b1, b2, b3, terms, rows):
    terms[...] = jnp.zeros_like(terms)
    for core, ref in enumerate((mine, other)):
        for zr in range(4):
            for q in range(4):
                at = zr * 256 + 128 + q * 32
                to = core * 128 + zr * 32
                rows[to : to + 32, q * 1024 : (q + 1) * 1024] = ref[at : at + 32]
    for j, ref in enumerate((b0, b1, b2, b3)):
        for i in range(4):
            for k in range(4):
                at_row, at_col, flag = place_of(slot_of(i, j, k, -1), row, col, live)
                term = jnp.dot(
                    rows[:, pl.ds(at_row, SIDE)], ref[i * 4 + k], preferred_element_type=F32
                )
                here = (slice(None), pl.ds(at_col, SIDE))
                terms[here] = terms[here] + term * flag


def slot_terms(row, col, live, mine, other, blocks, width):
    smem = pl.BlockSpec(memory_space=pltpu.SMEM)
    vmem = pl.BlockSpec(memory_space=pltpu.VMEM)
    return pl.pallas_call(
        terms_kernel,
        in_specs=[smem] * 3 + [vmem] * 6,
        out_specs=[vmem, vmem],
        out_shape=[struct((256, width), F32), struct((256, 4096), BF16)],
        cost_estimate=cost(64 * 2 * 256 * 128 * 128, 8 << 20),
    )(row, col, live, mine, other, *blocks)


def grads_kernel(factor, row, col, live, pre, own, a1, b1, a3, b3, held, g0, g1, g2, g3, dpre, flipped):
    for r in range(32):
        flipped[r * 128 : (r + 1) * 128] = held[:, r * 128 : (r + 1) * 128].T
    for core, (r1, r3) in enumerate(((a1, a3), (b1, b3))):
        rows = slice(core * 128, (core + 1) * 128)
        for n in range(pre.shape[1] // 256):
            at = slice(n * 256, (n + 1) * 256)
            back = own[rows, at].astype(F32) + r1[:, at].astype(F32)
            back = back + r3[:, at].astype(F32)
            value = pre[rows, at]
            sigma = jax.nn.sigmoid(value)
            dpre[rows, at] = (back * sigma * (1.0 + value * (1.0 - sigma))).astype(BF16)
    for i, out in enumerate((g0, g1, g2, g3)):
        for j in range(4):
            for k in range(4):
                at_row, at_col, flag = place_of(slot_of(i, j, k, 1), row, col, live)
                grad = jnp.dot(
                    flipped[pl.ds(at_row, SIDE), :],
                    dpre[:, pl.ds(at_col, SIDE)],
                    preferred_element_type=F32,
                )
                out[j * 4 + k] = (grad * (flag * factor)).astype(BF16)


def slot_grads(row, col, live, pre, back, held, factor):
    smem = pl.BlockSpec(memory_space=pltpu.SMEM)
    vmem = pl.BlockSpec(memory_space=pltpu.VMEM)

    def kernel(*refs):
        grads_kernel(factor, *refs)

    return pl.pallas_call(
        kernel,
        in_specs=[smem] * 3 + [vmem] * 7,
        out_specs=[vmem] * 4,
        out_shape=[struct((16, SIDE, SIDE), BF16)] * 4,
        scratch_shapes=[pltpu.VMEM(back[0].shape, BF16), pltpu.VMEM((4096, 256), BF16)],
        cost_estimate=cost(64 * 2 * 256 * 128 * 128, 8 << 20),
    )(row, col, live, pre, *back, held)


def finish_kernel(r0, r1, r2, r3, out):
    x, y = lax.axis_index("x"), lax.axis_index("y")
    for j, ref in enumerate((r0, r1, r2, r3)):
        for i in range(4):
            begin = pl.multiple_of(wrap(x - i) * 1024 + wrap(y + j) * 256, 256)
            out[:, pl.ds(begin, 256)] = ref[:, i * 256 : (i + 1) * 256]


def finish(pieces):
    return pl.pallas_call(
        finish_kernel,
        out_shape=struct((32, 4096), BF16),
        cost_estimate=cost(0, 1 << 19),
    )(*pieces)


def total_of(pieces):
    total = pieces[0].astype(F32)
    for piece in pieces[1:]:
        total = total + piece.astype(F32)
    return total


def on_device(
    tokens, cotangent, w_up, w_down, delta, first_moment, second_moment, blk_row, blk_col, live
):
    width = w_up.shape[1]
    up_pieces = ring(w_up, "y")
    sent_x, sent_c, chunks, block = prepare(tokens, cotangent, delta)
    unit = jnp.concatenate(exchange(sent_x, "x", 1), axis=0)
    x_mine = over_z(unit)
    x_other = swap_cores(x_mine)
    down_pieces = exchange([w_down] * 4, "x", 1)
    unit = jnp.concatenate(exchange(sent_c, "y", 1) + [chunks], axis=0)
    t_mine = over_z(unit)
    t_other = swap_cores(t_mine)
    column = exchange([block] * 4, "x", 1)
    column = jnp.concatenate(column, axis=0)
    blocks = exchange([column] * 4, "y", 1)
    terms, held = slot_terms(blk_row, blk_col, live, t_mine, t_other, blocks, width)

    pre_parts = ring_sum(up_partial(x_mine, x_other, up_pieces), "x")
    pre, h_mine, h_other = pre_and_hidden(pre_parts, terms)
    back = ring_sum(back_partial(t_mine, t_other, down_pieces), "y")

    a1, a3 = shift(h_other, "y", 1), shift(h_other, "y", -1)
    b1, b3 = shift(h_mine, "y", 1), shift(h_mine, "y", -1)
    a2, b2 = shift(a3, "y", -1), shift(b1, "y", 1)
    theirs = out_partial([h_other, a1, a2, a3], down_pieces)
    theirs = swap_cores(theirs)
    chip = out_partial([h_mine, b1, b2, b3], down_pieces, (theirs,))
    line = total_of(exchange(chip, "z", -1)).astype(BF16)
    layer_out = finish(exchange([line[k] for k in range(4)], "y", -1))

    factor = 1.0 / math.sqrt(4096.0)
    grads = slot_grads(blk_row, blk_col, live, pre, back, held, factor)
    row_sum = total_of(exchange(grads, "x", 1)).astype(BF16).reshape(4, 4, SIDE, SIDE)
    owned = total_of(exchange([row_sum[k] for k in range(4)], "y", 1))
    new_first = 0.9 * first_moment + 0.1 * owned
    new_second = 0.95 * second_moment + 0.05 * owned * owned
    corrected_first = new_first / (1.0 - 0.9**10)
    corrected_second = new_second / (1.0 - 0.95**10)
    new_delta = delta - 0.01 * corrected_first / (jnp.sqrt(corrected_second) + 1e-08)
    return (layer_out, new_delta, new_first, new_second)


def solution(mesh):
    split = Mesh(mesh.devices.reshape(4, 2, 4, 4), DEVICE)
    return jax.shard_map(
        on_device,
        mesh=split,
        in_specs=(
            P(DEVICE, None),
            P(DEVICE, None),
            P(SHARD, DP),
            P(DP, SHARD),
            P(DEVICE, None, None),
            P(DEVICE, None, None),
            P(DEVICE, None, None),
            P(),
            P(),
            P(),
        ),
        out_specs=(
            P(DEVICE, None),
            P(DEVICE, None, None),
            P(DEVICE, None, None),
            P(DEVICE, None, None),
        ),
        check_vma=False,
    )
```
